32 devices in a mesh: row: 8 (over y, x, core), col: 4 (over z).
Axes of the slice: x: 2, y: 2, z: 4, core: 2. Of those that a mesh axis runs over, the one named last changes fastest.
Arguments:
- inverse_rows: float32 [16384, 16384], P('col', 'row'), may hold values from -0.5 to 0.5
- panels: float32 [4, 16384, 256], P('col', 'row'), may hold values from -0.75 to 0.75
- diag_inverse: float32 [2, 256, 256], replicated, may hold values from -12 to 12
- pattern: int32 [2, 64], replicated, may hold values 0 or 1
- owner_slot: int32 [2], replicated, may hold values from 0 to 3, as said below
Outputs:
- inverse_column: float32 [2, 16384, 256], P(None, 'row')
- inverse_row: float32 [2, 256, 16384], P(None, None, 'col')
- diag_block: float32 [2, 256, 256], replicated
The draws below stay inside these ranges and needn't reach their ends.
Inputs may be any that keep to these rules, and one draw needn't show every extreme that they name: `owner_slot`: the two supernodes' panels lie in two different slots, one of them the last slot.
All inputs are finite; a program needn't handle non-finite values.
Results may differ from the reference program's by a relative error of at most 0.0001.
Values sent between devices are 32-bit elements; how exact they have to be, the bound alone decides.
A program may use at most 128 MiB of HBM per device.

```python
import jax
import jax.numpy as jnp
from jax import lax

W = 256
BLOCKS = 64
M = 16384
SLOTS = 4


def draw_owner_slot(key, part):
    first_key = jax.random.fold_in(key, 11)
    second_key = jax.random.fold_in(key, 23)
    other = jax.random.randint(first_key, (), 0, SLOTS - 1).astype(jnp.int32)
    flip = jax.random.randint(second_key, (), 0, 2).astype(jnp.int32)
    last = jnp.int32(SLOTS - 1)
    return jnp.where(flip == 1, jnp.stack([last, other]), jnp.stack([other, last])).astype(jnp.int32)


def touch_ends(result, stream_key, least, high):
    dims = result.shape
    index_at = [jax.random.randint(jax.random.fold_in(stream_key, axis), (), 0, dims[axis]) for axis in range(len(dims))]
    result = result.at[tuple(index_at)].set(least)
    longest = dims.index(max(dims))
    index_at[longest] = (index_at[longest] + 1) % dims[longest]
    return result.at[tuple(index_at)].set(high)


def raised(values, key, source, target, blocks, factor):
    owner, partner = [(jnp.arange(values.shape[dim]) // (values.shape[dim] // blocks)).reshape([-1 if axis == dim else 1 for axis in range(values.ndim)]) for dim in (source, target)]
    chosen = jax.random.permutation(key, blocks)[partner]
    strong = (owner == chosen) | (owner == (partner + blocks // 2) % blocks)
    return jnp.where(strong, factor * values, values)


def block_levels(key, shape, shards, smallest, largest):
    factor_of, own = 1.0, jax.random.fold_in(key, 6)
    for dim, shards_of in shards:
        draws = jnp.exp(jax.random.uniform(jax.random.fold_in(own, dim), (shards_of,), jnp.float32, smallest / len(shards), largest / len(shards)))
        factor_of = factor_of * jnp.repeat(draws, shape[dim] // shards_of).reshape([-1 if axis == dim else 1 for axis in range(len(shape))])
    return factor_of


def bell_draw(own_key, extent, scale, reach, shards=(), dtype=jnp.bfloat16):
    array = scale * jax.random.normal(own_key, extent, jnp.float32)
    if shards:
        array = array * block_levels(own_key, extent, shards, -0.22, 0.18)
    return jnp.clip(array, -reach, reach).astype(dtype)


def bell_draw_with(own_key, shape, scale, limit, cuts, heavy, dtype=jnp.bfloat16):
    values = scale * jax.random.normal(own_key, shape, jnp.float32)
    if cuts:
        values = values * block_levels(own_key, shape, cuts, -0.22, 0.18)
    return jnp.clip(raised(values, jax.random.fold_in(own_key, 3), *heavy), -limit, limit).astype(dtype)


def setup_inputs(seed: int = 0) -> dict:
    keys = jax.random.split(jax.random.key(seed), 6)
    return {
        "inverse_rows": bell_draw_with(keys[0], (M, M), (M // 64) ** -0.5, 0.5, ((0, 4), (1, 8)), (1, 0, 8, 2.0), jnp.float32),
        "panels": bell_draw(keys[1], (SLOTS, M, W), 0.125, 0.75, ((0, 4), (1, 8)), jnp.float32),
        "diag_inverse": bell_draw(keys[2], (2, W, W), 2.0, 12.0, (), jnp.float32),
        "pattern": touch_ends((jax.random.randint(keys[3], (2, BLOCKS), 0, 3) < 2).astype(jnp.int32), jax.random.fold_in(keys[3], 1), 0, 1),
        "owner_slot": draw_owner_slot(jax.random.fold_in(keys[5], 71), 0),
    }


def reference(inverse_rows, panels, diag_inverse, pattern, owner_slot):
    columns = []
    transposed = []
    diagonals = []
    for number in range(2):
        rowmask = jnp.repeat(pattern[number].astype(jnp.float32), W)
        chosen = lax.dynamic_index_in_dim(panels, owner_slot[number].astype(jnp.int32), 0, keepdims=False)
        masked = rowmask[:, None] * chosen
        product = jnp.dot(inverse_rows, masked, precision=lax.Precision.HIGHEST, preferred_element_type=jnp.float32)
        column = -(rowmask[:, None] * product)
        columns.append(column)
        transposed.append(column.T)
        inner = jnp.dot(masked.T, column, precision=lax.Precision.HIGHEST, preferred_element_type=jnp.float32)
        diagonals.append(diag_inverse[number] - inner)
    return jnp.stack(columns), jnp.stack(transposed), jnp.stack(diagonals)
```

```python
import functools

import jax
import jax.numpy as jnp
from jax import lax
from jax.experimental import pallas as pl
from jax.experimental.pallas import tpu as pltpu
from jax.sharding import PartitionSpec as P

MESH = pl.DeviceIdType.MESH
F32 = jnp.float32
BF16 = jnp.bfloat16
CHUNKS = 8
TILES = 16


def halves(x):
    high = x.astype(BF16)
    return high, (x - high.astype(F32)).astype(BF16)


def dot3(a, b):
    (ah, al), (bh, bl) = a, b
    out = jnp.dot(ah, bh, preferred_element_type=F32)
    out += jnp.dot(ah, bl, preferred_element_type=F32)
    out += jnp.dot(al, bh, preferred_element_type=F32)
    return out


def kernel(
    n_rows, n_cols,
    a_ref, own_last, own_other, sign_ref, dinv_ref,
    y_out, low_out, diag_out,
    bf, bh, bl, plus, minus, part, y, low, abuf, dpart, dsum, *rest,
):
    bits = n_rows.bit_length() - 1
    rs_buf, d_buf = rest[:bits], rest[bits:2 * bits]
    (last_s, last_r, plus_s, plus_r, minus_s, minus_r, rs_s, rs_r, ag_s, ag_r,
     zl_s, zr_s, z_r, a_sem, o_sem) = rest[2 * bits:]
    r = lax.axis_index("row")
    c = lax.axis_index("col")
    width = bf.shape[2]
    depth = bf.shape[1]
    rows = y.shape[1]
    ch = depth // CHUNKS
    tm = rows // TILES
    end = n_cols - 1
    core = lax.rem(r, 2)
    left, right = {"col": c - 1}, {"col": c + 1}

    def bit_of(j):
        if j == 0:
            return 1
        return (1 << j) + core * ((1 << (bits - j)) - (1 << j))

    value = [lax.rem(lax.div(r, bit_of(j)), 2) for j in range(bits)]
    partner = [r + (1 - 2 * value[j]) * bit_of(j) for j in range(bits)]

    def starts(total):
        out = [0]
        for j in range(bits):
            out.append(out[-1] + value[j] * (total >> (j + 1)))
        return out

    def span(start, size):
        return pl.ds(pl.multiple_of(start, 8), size)

    def chunk(k):
        return span(k * ch, ch)

    def remote(src, dst, send, recv, where):
        return pltpu.make_async_remote_copy(
            src_ref=src, dst_ref=dst, send_sem=send, recv_sem=recv,
            device_id=where, device_id_type=MESH,
        )

    def a_copy(g):
        t = lax.rem(g, TILES)
        start = lax.rem(t * tm + (1 - value[0]) * (rows // 2), rows)
        slot = lax.rem(g, 2)
        return start, slot, pltpu.make_async_copy(
            a_ref.at[span(start, tm), :], abuf.at[slot], a_sem.at[slot]
        )

    def multiply(s, t):
        g = s * TILES + t
        start, slot, copy = a_copy(g)

        @pl.when(g + 1 < 2 * TILES)
        def _():
            a_copy(g + 1)[2].start()

        copy.wait()
        total = None
        step = min(512, depth)
        for k in range(0, depth, step):
            a = halves(abuf[slot, :, k:k + step])
            term = dot3(a, (bh[s, k:k + step, :], bl[s, k:k + step, :]))
            total = term if total is None else total + term
        part[s, span(start, tm), :] = total

    def loop(low_, high_, body):
        def step(i, carry):
            body(i)
            return carry
        lax.fori_loop(low_, high_, step, 0)

    def split(s, k):
        high, rest_ = halves(bf[s, chunk(k), :])
        bh[s, chunk(k), :] = high
        bl[s, chunk(k), :] = rest_

    def last_copy(k, src):
        return remote(src, bf.at[0, chunk(k), :], last_s.at[k], last_r.at[k], left)

    def plus_copy(k, src):
        return remote(src, plus.at[chunk(k), :], plus_s.at[k], plus_r.at[k], right)

    def minus_copy(k, src):
        return remote(src, minus.at[chunk(k), :], minus_s.at[k], minus_r.at[k], left)

    def first_phase(k):
        here = chunk(k)

        @pl.when(c == end)
        def _():
            bf[0, here, :] = own_last[here, :]

        @pl.when(c < end)
        def _():
            last_copy(k, bf.at[0, here, :]).wait_recv()

        @pl.when((c < end) & (c > 0))
        def _():
            last_copy(k, bf.at[0, here, :]).start()

        split(0, k)

        @pl.when(c == 0)
        def _():
            plus[here, :] = own_other[here, :]

        @pl.when(c > 0)
        def _():
            plus_copy(k, plus.at[here, :]).wait_recv()
            plus[here, :] = plus[here, :] + own_other[here, :]

        @pl.when((c > 0) & (c < end))
        def _():
            plus_copy(k, plus.at[here, :]).start()

    def second_phase(k):
        here = chunk(k)

        @pl.when(c < end - 1)
        def _():
            minus_copy(k, minus.at[here, :]).wait_recv()
            arrived = minus[here, :]
            bf[1, here, :] = plus[here, :] + arrived
            minus[here, :] = arrived + own_other[here, :]

        @pl.when((c < end - 1) & (c > 0))
        def _():
            minus_copy(k, minus.at[here, :]).start()

        @pl.when(c >= end - 1)
        def _():
            bf[1, here, :] = plus[here, :]

        @pl.when((c == end - 1) & (c > 0))
        def _():
            minus_copy(k, own_other.at[here, :]).start()

        split(1, k)

    def reduce_events(s, src, bufs, dst, total, finish):
        start = starts(total)
        size = [total >> j for j in range(bits + 1)]

        def rs(j):
            away = start[j] + (1 - value[j]) * size[j + 1]
            return remote(src.at[span(away, size[j + 1]), :], bufs[j],
                          rs_s.at[s, j], rs_r.at[s, j], {"row": partner[j]})

        def ag(j):
            mine = span(start[j + 1], size[j + 1])
            return remote(dst.at[mine, :], dst.at[mine, :],
                          ag_s.at[s, j], ag_r.at[s, j], {"row": partner[j]})

        def add(j):
            rs(j).wait()
            mine = size[j + 1]
            piece = min(mine, 128)

            def body(i):
                here = span(start[j + 1] + i * piece, piece)
                src[here, :] = src[here, :] + bufs[j][span(i * piece, piece), :]
            loop(0, mine // piece, body)

        def event(i):
            if i == 0:
                rs(0).start()
            elif i < bits:
                add(i - 1)
                rs(i).start()
            elif i == bits:
                add(bits - 1)
                finish(start[bits], size[bits])
                ag(bits - 1).start()
            else:
                j = 2 * bits - i
                ag(j).wait()
                if j > 0:
                    ag(j - 1).start()
        return [functools.partial(event, i) for i in range(2 * bits + 1)]

    def finish_column(s, start, size):
        piece = min(size, width, 128)

        def body(i):
            at = start + i * piece
            block = lax.div(c * rows + at, width)
            here = span(at, piece)
            y[s, here, :] = sign_ref[s, block] * part[s, here, :]
        loop(0, size // piece, body)

    source = lax.div(r * n_cols, n_rows)
    own_start = r * depth - source * rows

    def z_copy(s, k, src, way):
        sem = zl_s if way < 0 else zr_s
        return remote(src, low.at[s, chunk(k), :], sem.at[s, k], z_r.at[s, k],
                      left if way < 0 else right)

    def z_send(s, k, src):
        @pl.when((c <= source) & (c > 0))
        def _():
            z_copy(s, k, src, -1).start()

        @pl.when((c >= source) & (c < end))
        def _():
            z_copy(s, k, src, 1).start()

    def z_root(s):
        @pl.when(c == source)
        def _():
            def send(k):
                z_send(s, k, y.at[s, span(own_start + k * ch, ch), :])
            loop(0, CHUNKS, send)

            def keep(k):
                low[s, chunk(k), :] = y[s, span(own_start + k * ch, ch), :]
            loop(0, CHUNKS, keep)

    def z_relay(s, k):
        @pl.when(c != source)
        def _():
            z_copy(s, k, low.at[s, chunk(k), :], 1).wait_recv()
            z_send(s, k, low.at[s, chunk(k), :])

    def y_copy(s):
        return pltpu.make_async_copy(y.at[s], y_out.at[s], o_sem.at[s])

    def low_copy(s):
        return pltpu.make_async_copy(low.at[s], low_out.at[s], o_sem.at[2 + s])

    def inner(s, k):
        b = halves(bf[s, chunk(k), :].T)
        here = pl.ds(s * width, width)
        dpart[here, :] += dot3(b, halves(low[s, chunk(k), :]))

    barrier = pltpu.get_barrier_semaphore()
    for j in range(bits):
        pl.semaphore_signal(barrier, inc=1, device_id={"row": partner[j]}, device_id_type=MESH)

    @pl.when(c > 0)
    def _():
        pl.semaphore_signal(barrier, inc=1, device_id=left, device_id_type=MESH)

    @pl.when(c < end)
    def _():
        pl.semaphore_signal(barrier, inc=1, device_id=right, device_id_type=MESH)

    beside = lax.div(c + end - 1, end) + lax.div(2 * end - 1 - c, end)
    pl.semaphore_wait(barrier, bits + beside)

    a_copy(0)[2].start()

    @pl.when(c == end)
    def _():
        loop(0, CHUNKS, lambda k: last_copy(k, own_last.at[chunk(k), :]).start())

    @pl.when(c == 0)
    def _():
        loop(0, CHUNKS, lambda k: plus_copy(k, own_other.at[chunk(k), :]).start())

    loop(0, CHUNKS, first_phase)

    first = reduce_events(0, part.at[0], [b.at[0] for b in rs_buf], y.at[0], rows,
                          functools.partial(finish_column, 0))
    second = reduce_events(1, part.at[1], [b.at[1] for b in rs_buf], y.at[1], rows,
                           functools.partial(finish_column, 1))

    def finish_diag(start, size):
        here = span(start, size)
        dsum[here, :] = dpart[here, :]

    third = reduce_events(2, dpart, d_buf, dsum, 2 * width, finish_diag)

    def both(k):
        second_phase(k)
        loop(0, 4, lambda i: multiply(0, 4 * k + i))

    loop(0, 2, both)
    first[0]()
    loop(2, 4, both)
    todo = list(first[1:])
    for k in range(4, CHUNKS):
        second_phase(k)
        if todo:
            todo.pop(0)()
    loop(0, 4, lambda t: multiply(1, t))
    if todo:
        todo.pop(0)()
    loop(4, 8, lambda t: multiply(1, t))
    second[0]()
    for event in todo:
        event()
    z_root(0)
    y_copy(0).start()
    loop(8, 16, lambda t: multiply(1, t))
    rest_events = second[1:]
    done = 0
    for i, event in enumerate(rest_events):
        event()
        upto = CHUNKS * (i + 1) // len(rest_events)
        for k in range(done, upto):
            z_relay(0, k)
        done = upto
    z_root(1)
    y_copy(1).start()
    low_copy(0).start()
    dpart[...] = jnp.zeros_like(dpart)
    loop(0, CHUNKS, lambda k: inner(0, k))

    def tail(k):
        z_relay(1, k)
        inner(1, k)
    loop(0, CHUNKS, tail)
    low_copy(1).start()
    for event in third:
        event()
    diag_out[...] = dinv_ref[...] - dsum[...]

    def drain(k):
        here = chunk(k)

        @pl.when(c > 0)
        def _():
            last_copy(k, own_last.at[here, :]).wait_send()

        @pl.when(c < end)
        def _():
            plus_copy(k, plus.at[here, :]).wait_send()

        @pl.when((c < end) & (c > 0))
        def _():
            minus_copy(k, minus.at[here, :]).wait_send()

        for s in range(2):
            src = low.at[s, here, :]

            @pl.when((c <= source) & (c > 0))
            def _():
                z_copy(s, k, src, -1).wait_send()

            @pl.when((c >= source) & (c < end))
            def _():
                z_copy(s, k, src, 1).wait_send()
    loop(0, CHUNKS, drain)
    for s in range(2):
        y_copy(s).wait()
        low_copy(s).wait()


def exchange(n_rows, n_cols, a, own_last, own_other, sign, dinv):
    rows, depth = a.shape
    width = own_last.shape[1]
    bits = n_rows.bit_length() - 1
    vmem = pl.BlockSpec(memory_space=pltpu.VMEM)
    anywhere = pl.BlockSpec(memory_space=pl.ANY)
    dma = pltpu.SemaphoreType.DMA
    n = CHUNKS
    return pl.pallas_call(
        functools.partial(kernel, n_rows, n_cols),
        out_shape=(
            jax.ShapeDtypeStruct((2, rows, width), F32),
            jax.ShapeDtypeStruct((2, depth, width), F32),
            jax.ShapeDtypeStruct((2 * width, width), F32),
        ),
        in_specs=[anywhere, vmem, vmem, pl.BlockSpec(memory_space=pltpu.SMEM), vmem],
        out_specs=(anywhere, anywhere, vmem),
        scratch_shapes=[
            pltpu.VMEM((2, depth, width), F32),
            pltpu.VMEM((2, depth, width), BF16),
            pltpu.VMEM((2, depth, width), BF16),
            pltpu.VMEM((depth, width), F32),
            pltpu.VMEM((depth, width), F32),
            pltpu.VMEM((2, rows, width), F32),
            pltpu.VMEM((2, rows, width), F32),
            pltpu.VMEM((2, depth, width), F32),
            pltpu.VMEM((2, rows // TILES, depth), F32),
            pltpu.VMEM((2 * width, width), F32),
            pltpu.VMEM((2 * width, width), F32),
            *[pltpu.VMEM((2, rows >> (j + 1), width), F32) for j in range(bits)],
            *[pltpu.VMEM((2 * width >> (j + 1), width), F32) for j in range(bits)],
            dma((n,)), dma((n,)), dma((n,)), dma((n,)), dma((n,)), dma((n,)),
            dma((3, bits)), dma((3, bits)), dma((3, bits)), dma((3, bits)),
            dma((2, n)), dma((2, n)), dma((2, n)),
            dma((2,)), dma((4,)),
        ],
        compiler_params=pltpu.CompilerParams(
            collective_id=0, has_side_effects=True, vmem_limit_bytes=66_000_000
        ),
    )(a, own_last, own_other, sign, dinv)


def shards(inverse_rows, panels, diag_inverse, pattern, owner_slot):
    n_rows = lax.axis_size("row")
    n_cols = lax.axis_size("col")
    row_index = lax.axis_index("row")
    col_index = lax.axis_index("col")
    width = panels.shape[2]
    blocks_here = pattern.shape[1] // n_rows
    flip = (owner_slot[0] != n_cols - 1).astype(jnp.int32)
    order = (flip, 1 - flip)
    live = jnp.stack([lax.dynamic_index_in_dim(pattern, o, 0, keepdims=False) for o in order])
    live = live.astype(F32)
    mask = lax.dynamic_slice_in_dim(live, row_index * blocks_here, blocks_here, 1)
    mask = jnp.repeat(mask, width, axis=1)[:, :, None]
    own_last = mask[0] * panels[0]
    mine = owner_slot[order[1]] == col_index
    own_other = jnp.where(mine, mask[1] * panels[0], 0.0)
    dinv = jnp.concatenate(
        [lax.dynamic_index_in_dim(diag_inverse, o, 0, keepdims=False) for o in order]
    )
    y, low, diag = exchange(n_rows, n_cols, inverse_rows, own_last, own_other, -live, dinv)

    def back(x):
        return jnp.stack([lax.dynamic_index_in_dim(x, o, 0, keepdims=False) for o in order])
    return back(low), jnp.swapaxes(back(y), 1, 2), back(diag.reshape(2, width, width))


def solution(mesh):
    in_specs = (P("col", "row"), P("col", "row", None), P(), P(), P())
    out_specs = (P(None, "row", None), P(None, None, "col"), P())
    return jax.shard_map(shards, mesh=mesh, in_specs=in_specs, out_specs=out_specs, check_vma=False)
```

```python
import functools

import jax
import jax.numpy as jnp
from jax import lax
from jax.experimental import pallas as pl
from jax.experimental.pallas import tpu as pltpu
from jax.sharding import PartitionSpec as P

MESH = pl.DeviceIdType.MESH
F32 = jnp.float32
BF16 = jnp.bfloat16
CHUNKS = 16
TILES = 16


def halves(x):
    high = x.astype(BF16)
    return high, (x - high.astype(F32)).astype(BF16)


def dot3(a, b):
    (ah, al), (bh, bl) = a, b
    out = jnp.dot(ah, bh, preferred_element_type=F32)
    out += jnp.dot(ah, bl, preferred_element_type=F32)
    out += jnp.dot(al, bh, preferred_element_type=F32)
    return out


def weave(one, two):
    keyed = [((i + 0.5) / len(x), n, f) for n, x in enumerate((one, two)) for i, f in enumerate(x)]
    return [f for _, _, f in sorted(keyed, key=lambda item: item[:2])]


def kernel(
    n_rows, n_cols,
    a_ref, panel, scale_ref, sign_ref, dinv_ref,
    y_out, low_out, diag_out,
    bf, bh, bl, plus, minus, part, y, low, abuf, turned, dpart, dsum, *rest,
):
    bits = n_rows.bit_length() - 1
    rs_buf, d_buf = rest[:bits], rest[bits:2 * bits]
    (plus_s, plus_r, minus_s, minus_r, rs_s, rs_r, ag_s, ag_r,
     zl_s, zr_s, z_r, a_sem, t_sem, o_sem) = rest[2 * bits:]
    r = lax.axis_index("row")
    c = lax.axis_index("col")
    width = bf.shape[2]
    depth = bf.shape[1]
    rows = y.shape[1]
    ch = depth // CHUNKS
    tm = rows // TILES
    strip = rows // 4
    end = n_cols - 1
    core = lax.rem(r, 2)
    left, right = {"col": c - 1}, {"col": c + 1}

    def bit_of(j):
        if j == 0:
            return 1
        return (1 << j) + core * ((1 << (bits - j)) - (1 << j))

    value = [lax.rem(lax.div(r, bit_of(j)), 2) for j in range(bits)]
    partner = [r + (1 - 2 * value[j]) * bit_of(j) for j in range(bits)]

    def span(start, size):
        return pl.ds(pl.multiple_of(start, 8), size)

    def chunk(k):
        return span(k * ch, ch)

    def remote(src, dst, send, recv, where):
        return pltpu.make_async_remote_copy(
            src_ref=src, dst_ref=dst, send_sem=send, recv_sem=recv,
            device_id=where, device_id_type=MESH,
        )

    def loop(low_, high_, body):
        def step(i, carry):
            body(i)
            return carry
        lax.fori_loop(low_, high_, step, 0)

    def a_copy(g):
        t = lax.rem(g, TILES)
        quarter = lax.div(t, TILES // 4)
        half = (1 - value[0]) + lax.rem(quarter, 2) * (2 * value[0] - 1)
        start = (lax.div(quarter, 2) * strip + half * (rows // 2)
                 + lax.rem(t, TILES // 4) * tm)
        slot = lax.rem(g, 2)
        return start, slot, pltpu.make_async_copy(
            a_ref.at[span(start, tm), :], abuf.at[slot], a_sem.at[slot]
        )

    def multiply(s, t):
        g = s * TILES + t
        start, slot, copy = a_copy(g)

        @pl.when(g + 1 < 2 * TILES)
        def _():
            a_copy(g + 1)[2].start()

        copy.wait()
        total = None
        step = min(512, depth)
        for k in range(0, depth, step):
            a = halves(abuf[slot, :, k:k + step])
            term = dot3(a, (bh[s, k:k + step, :], bl[s, k:k + step, :]))
            total = term if total is None else total + term
        part[s, span(start, tm), :] = total

    def plus_copy(s, k):
        ref = plus.at[s, chunk(k), :]
        return remote(ref, ref, plus_s.at[s, k], plus_r.at[s, k], right)

    def minus_copy(s, k):
        ref = minus.at[s, chunk(k), :]
        return remote(ref, ref, minus_s.at[s, k], minus_r.at[s, k], left)

    def own(s, k):
        block = lax.div(r * depth + k * ch, width)
        return scale_ref[s, block] * panel[chunk(k), :]

    total_chunks = 2 * CHUNKS

    def panel_step(j):
        up = j - c

        @pl.when((up >= 0) & (up < total_chunks))
        def _():
            s, k = lax.div(up, CHUNKS), lax.rem(up, CHUNKS)

            @pl.when(c > 0)
            def _():
                plus_copy(s, k).wait_recv()
                plus[s, chunk(k), :] = plus[s, chunk(k), :] + own(s, k)

            @pl.when(c == 0)
            def _():
                plus[s, chunk(k), :] = own(s, k)

            @pl.when(c < end)
            def _():
                plus_copy(s, k).start()

        down = j - (end - c)

        @pl.when((down >= 0) & (down < total_chunks))
        def _():
            s, k = lax.div(down, CHUNKS), lax.rem(down, CHUNKS)

            @pl.when(c < end)
            def _():
                minus_copy(s, k).wait_recv()
                minus[s, chunk(k), :] = minus[s, chunk(k), :] + own(s, k)

            @pl.when(c == end)
            def _():
                minus[s, chunk(k), :] = own(s, k)

            @pl.when(c > 0)
            def _():
                minus_copy(s, k).start()

        at = j - end

        @pl.when(at >= 0)
        def _():
            s, k = lax.div(at, CHUNKS), lax.rem(at, CHUNKS)
            x = (plus[s, chunk(k), :] + minus[s, chunk(k), :]) - own(s, k)
            bf[s, chunk(k), :] = x
            high, rest_ = halves(x)
            bh[s, chunk(k), :] = high
            bl[s, chunk(k), :] = rest_

    def reduce_events(g, src, bufs, dst, apart, offset, first_size, finish):
        size = [None] + [first_size >> j for j in range(bits)]
        start = [None, value[0] * apart + offset]
        for j in range(1, bits):
            start.append(start[-1] + value[j] * size[j + 1])

        def away(j):
            if j == 0:
                return (1 - value[0]) * apart + offset
            return start[j] + (1 - value[j]) * size[j + 1]

        def rs(j):
            return remote(src.at[span(away(j), size[j + 1]), :], bufs[j],
                          rs_s.at[g, j], rs_r.at[g, j], {"row": partner[j]})

        def ag(j):
            if j == 0:
                mine = span(start[1], size[1])
            else:
                mine = span(start[j + 1], size[j + 1])
            return remote(dst.at[mine, :], dst.at[mine, :],
                          ag_s.at[g, j], ag_r.at[g, j], {"row": partner[j]})

        def add(j):
            rs(j).wait()
            mine = size[j + 1]
            piece = min(mine, 128)

            def body(i):
                here = span(start[j + 1] + i * piece, piece)
                src[here, :] = src[here, :] + bufs[j][span(i * piece, piece), :]
            loop(0, mine // piece, body)

        def event(i):
            if i == 0:
                rs(0).start()
            elif i < bits:
                add(i - 1)
                rs(i).start()
            elif i == bits:
                add(bits - 1)
                finish(start[bits], size[bits])
                ag(bits - 1).start()
            else:
                j = 2 * bits - i
                ag(j).wait()
                if j > 0:
                    ag(j - 1).start()
        return [functools.partial(event, i) for i in range(2 * bits + 1)]

    def finish_column(s, start, size):
        piece = min(size, width, 128)

        def body(i):
            at = start + i * piece
            block = lax.div(c * rows + at, width)
            here = span(at, piece)
            y[s, here, :] = sign_ref[s, block] * part[s, here, :]
        loop(0, size // piece, body)

    source = lax.div(r * n_cols, n_rows)
    own_start = r * depth - source * rows
    parts = [[k for k in range(CHUNKS) if (k * ch // strip) % 2 == h] for h in range(2)]

    def z_copy(s, k, src, way):
        sem = zl_s if way < 0 else zr_s
        return remote(src, low.at[s, chunk(k), :], sem.at[s, k], z_r.at[s, k],
                      left if way < 0 else right)

    def z_send(s, k, src):
        @pl.when((c <= source) & (c > 0))
        def _():
            z_copy(s, k, src, -1).start()

        @pl.when((c >= source) & (c < end))
        def _():
            z_copy(s, k, src, 1).start()

    def z_root(s, h):
        @pl.when(c == source)
        def _():
            for k in parts[h]:
                z_send(s, k, y.at[s, span(own_start + k * ch, ch), :])
            for k in parts[h]:
                low[s, chunk(k), :] = y[s, span(own_start + k * ch, ch), :]

    def z_relay(s, k):
        @pl.when(c != source)
        def _():
            z_copy(s, k, low.at[s, chunk(k), :], 1).wait_recv()
            z_send(s, k, low.at[s, chunk(k), :])

    def low_copy(s):
        return pltpu.make_async_copy(low.at[s], low_out.at[s], o_sem.at[s])

    tb = rows // 8

    def turn_copy(i):
        s, b = i // 8, i % 8
        return pltpu.make_async_copy(
            turned.at[i % 2], y_out.at[s, :, pl.ds(b * tb, tb)], t_sem.at[i % 2]
        )

    def turn(i):
        s, b = i // 8, i % 8
        if i >= 2:
            turn_copy(i - 2).wait()
        turned[i % 2] = y[s, pl.ds(b * tb, tb), :].T
        turn_copy(i).start()

    def inner(s, k):
        b = halves(bf[s, chunk(k), :].T)
        dpart[s] += dot3(b, halves(low[s, chunk(k), :]))

    barrier = pltpu.get_barrier_semaphore()
    for j in range(bits):
        pl.semaphore_signal(barrier, inc=1, device_id={"row": partner[j]}, device_id_type=MESH)

    @pl.when(c > 0)
    def _():
        pl.semaphore_signal(barrier, inc=1, device_id=left, device_id_type=MESH)

    @pl.when(c < end)
    def _():
        pl.semaphore_signal(barrier, inc=1, device_id=right, device_id_type=MESH)

    beside = lax.div(c + end - 1, end) + lax.div(2 * end - 1 - c, end)
    pl.semaphore_wait(barrier, bits + beside)

    a_copy(0)[2].start()
    dpart[...] = jnp.zeros_like(dpart)

    def column_events(s, h):
        g = 2 * s + h
        return reduce_events(g, part.at[s], [b.at[g] for b in rs_buf], y.at[s],
                             rows // 2, h * strip, strip, functools.partial(finish_column, s))

    def diag_events(s):
        def finish(start, size):
            here = span(start, size)
            dsum[s, here, :] = dpart[s, here, :]
        return reduce_events(4 + s, dpart.at[s], [b.at[s] for b in d_buf], dsum.at[s],
                             width // 2, 0, width // 2, finish)

    events = {(s, h): column_events(s, h) for s in range(2) for h in range(2)}
    root = {key: functools.partial(z_root, *key) for key in events}
    ready = CHUNKS + end
    quarter = TILES // 4

    loop(0, ready, panel_step)
    per = CHUNKS // 2 // 4
    for q in range(4):
        def both(i, q=q):
            panel_step(ready + q * per + i)
            each = quarter // per
            loop(0, each, lambda m: multiply(0, q * quarter + i * each + m))
        loop(0, per, both)
        e, f = events[0, 0], events[0, 1]
        for event in ([e[0]], [e[1]], [f[0]], [e[2], f[1]])[q]:
            event()
    steps = [functools.partial(panel_step, ready + 4 * per + i) for i in range(CHUNKS - 4 * per)]
    e, f = events[0, 0][3:] + [root[0, 0]], events[0, 1][2:] + [root[0, 1]]
    late = 2
    for step in weave(steps, weave(e, f[:-late])):
        step()
    order = parts[0] + parts[1]
    relays = [functools.partial(z_relay, 0, k) for k in order]
    for q in range(4):
        loop(0, quarter, lambda m: multiply(1, q * quarter + m))
        e, g = events[1, 0], events[1, 1]
        if q == 0:
            todo = f[-late:] + [e[0]]
        else:
            todo = relays[:2] + [[], [e[1]], [g[0]], [e[2], g[1]]][q]
            relays = relays[2:]
        for event in todo:
            event()
    e, g = events[1, 0][3:] + [root[1, 0]], events[1, 1][2:] + [root[1, 1]]
    for step in weave(weave(e, g), relays):
        step()
    low_copy(0).start()
    inners = [functools.partial(loop, i * CHUNKS // 4, (i + 1) * CHUNKS // 4,
                                lambda k: inner(0, k)) for i in range(4)]
    side = weave(inners + diag_events(0), [functools.partial(turn, i) for i in range(16)])

    def last(k):
        z_relay(1, k)
        inner(1, k)
    for step in weave([functools.partial(last, k) for k in order], side):
        step()
    low_copy(1).start()
    for event in diag_events(1):
        event()
    diag_out[...] = dinv_ref[...] - dsum[...]

    for s in range(2):
        def drain(k, s=s):
            @pl.when(c < end)
            def _():
                plus_copy(s, k).wait_send()

            @pl.when(c > 0)
            def _():
                minus_copy(s, k).wait_send()

            src = low.at[s, chunk(k), :]

            @pl.when((c <= source) & (c > 0))
            def _():
                z_copy(s, k, src, -1).wait_send()

            @pl.when((c >= source) & (c < end))
            def _():
                z_copy(s, k, src, 1).wait_send()
        loop(0, CHUNKS, drain)
    turn_copy(14).wait()
    turn_copy(15).wait()
    for s in range(2):
        low_copy(s).wait()


def exchange(n_rows, n_cols, a, panel, scale, sign, dinv):
    rows, depth = a.shape
    width = panel.shape[1]
    bits = n_rows.bit_length() - 1
    vmem = pl.BlockSpec(memory_space=pltpu.VMEM)
    smem = pl.BlockSpec(memory_space=pltpu.SMEM)
    anywhere = pl.BlockSpec(memory_space=pl.ANY)
    dma = pltpu.SemaphoreType.DMA
    n = CHUNKS
    return pl.pallas_call(
        functools.partial(kernel, n_rows, n_cols),
        out_shape=(
            jax.ShapeDtypeStruct((2, width, rows), F32),
            jax.ShapeDtypeStruct((2, depth, width), F32),
            jax.ShapeDtypeStruct((2, width, width), F32),
        ),
        in_specs=[anywhere, vmem, smem, smem, vmem],
        out_specs=(anywhere, anywhere, vmem),
        scratch_shapes=[
            pltpu.VMEM((2, depth, width), F32),
            pltpu.VMEM((2, depth, width), BF16),
            pltpu.VMEM((2, depth, width), BF16),
            pltpu.VMEM((2, depth, width), F32),
            pltpu.VMEM((2, depth, width), F32),
            pltpu.VMEM((2, rows, width), F32),
            pltpu.VMEM((2, rows, width), F32),
            pltpu.VMEM((2, depth, width), F32),
            pltpu.VMEM((2, rows // TILES, depth), F32),
            pltpu.VMEM((2, width, rows // 8), F32),
            pltpu.VMEM((2, width, width), F32),
            pltpu.VMEM((2, width, width), F32),
            *[pltpu.VMEM((4, rows // 4 >> j, width), F32) for j in range(bits)],
            *[pltpu.VMEM((2, width // 2 >> j, width), F32) for j in range(bits)],
            dma((2, n)), dma((2, n)), dma((2, n)), dma((2, n)),
            dma((6, bits)), dma((6, bits)), dma((6, bits)), dma((6, bits)),
            dma((2, n)), dma((2, n)), dma((2, n)),
            dma((2,)), dma((2,)), dma((2,)),
        ],
        compiler_params=pltpu.CompilerParams(
            collective_id=0, has_side_effects=True, vmem_limit_bytes=66_000_000
        ),
    )(a, panel, scale, sign, dinv)


def shards(inverse_rows, panels, diag_inverse, pattern, owner_slot):
    live = pattern.astype(F32)
    mine = (owner_slot == lax.axis_index("col")).astype(F32)
    y, low, diag = exchange(
        lax.axis_size("row"), lax.axis_size("col"), inverse_rows, panels[0],
        live * mine[:, None], -live, diag_inverse,
    )
    return low, y, diag


def solution(mesh):
    in_specs = (P("col", "row"), P("col", "row", None), P(), P(), P())
    out_specs = (P(None, "row", None), P(None, None, "col"), P())
    return jax.shard_map(shards, mesh=mesh, in_specs=in_specs, out_specs=out_specs, check_vma=False)
```

```python
import functools

import jax
import jax.numpy as jnp
from jax import lax
from jax.experimental import pallas as pl
from jax.experimental.pallas import tpu as pltpu
from jax.sharding import PartitionSpec as P

MESH = pl.DeviceIdType.MESH
F32 = jnp.float32
BF16 = jnp.bfloat16
CHUNKS = 16
TILES = 16
AHEAD = 3


def halves(x):
    high = x.astype(BF16)
    return high, (x - high.astype(F32)).astype(BF16)


def dot3(a, b):
    (ah, al), (bh, bl) = a, b
    out = jnp.dot(ah, bh, preferred_element_type=F32)
    out += jnp.dot(ah, bl, preferred_element_type=F32)
    out += jnp.dot(al, bh, preferred_element_type=F32)
    return out


def weave(one, two):
    keyed = [((i + 0.5) / len(x), n, f) for n, x in enumerate((one, two)) for i, f in enumerate(x)]
    return [f for _, _, f in sorted(keyed, key=lambda item: item[:2])]


def kernel(
    n_rows, n_cols,
    a_ref, panel, scale_ref, sign_ref, dinv_ref,
    y_out, low_out, diag_out,
    bf, bh, bl, plus, minus, part, y, low, abuf, turned, dpart, dsum, *rest,
):
    bits = n_rows.bit_length() - 1
    rs_buf, d_buf = rest[:bits], rest[bits:2 * bits]
    (plus_s, plus_r, minus_s, minus_r, rs_s, rs_r, ag_s, ag_r,
     zl_s, zr_s, z_r, a_sem, t_sem, o_sem) = rest[2 * bits:]
    r = lax.axis_index("row")
    c = lax.axis_index("col")
    width = bf.shape[2]
    depth = bf.shape[1]
    rows = y.shape[1]
    ch = depth // CHUNKS
    tm = rows // TILES
    strip = rows // 4
    end = n_cols - 1
    core = lax.rem(r, 2)
    left, right = {"col": c - 1}, {"col": c + 1}

    def bit_of(j):
        if j == 0:
            return 1
        return (1 << j) + core * ((1 << (bits - j)) - (1 << j))

    value = [lax.rem(lax.div(r, bit_of(j)), 2) for j in range(bits)]
    partner = [r + (1 - 2 * value[j]) * bit_of(j) for j in range(bits)]

    def span(start, size):
        return pl.ds(pl.multiple_of(start, 8), size)

    def chunk(k):
        return span(k * ch, ch)

    def remote(src, dst, send, recv, where):
        return pltpu.make_async_remote_copy(
            src_ref=src, dst_ref=dst, send_sem=send, recv_sem=recv,
            device_id=where, device_id_type=MESH,
        )

    def loop(low_, high_, body):
        def step(i, carry):
            body(i)
            return carry
        lax.fori_loop(low_, high_, step, 0)

    def a_copy(g):
        t = lax.rem(g, TILES)
        quarter = lax.div(t, TILES // 4)
        half = (1 - value[0]) + lax.rem(quarter, 2) * (2 * value[0] - 1)
        start = (lax.div(quarter, 2) * strip + half * (rows // 2)
                 + lax.rem(t, TILES // 4) * tm)
        slot = lax.rem(g, 2)
        return start, slot, pltpu.make_async_copy(
            a_ref.at[span(start, tm), :], abuf.at[slot], a_sem.at[slot]
        )

    def multiply(s, t):
        g = s * TILES + t
        start, slot, copy = a_copy(g)

        @pl.when(g + 1 < 2 * TILES)
        def _():
            a_copy(g + 1)[2].start()

        copy.wait()
        total = None
        step = min(512, depth)
        for k in range(0, depth, step):
            a = halves(abuf[slot, :, k:k + step])
            term = dot3(a, (bh[s, k:k + step, :], bl[s, k:k + step, :]))
            total = term if total is None else total + term
        part[s, span(start, tm), :] = total

    def plus_copy(s, k):
        ref = plus.at[s, chunk(k), :]
        return remote(ref, ref, plus_s.at[s, k], plus_r.at[s, k], right)

    def minus_copy(s, k):
        ref = minus.at[s, chunk(k), :]
        return remote(ref, ref, minus_s.at[s, k], minus_r.at[s, k], left)

    def own(s, k):
        block = lax.div(r * depth + k * ch, width)
        return scale_ref[s, block] * panel[chunk(k), :]

    total_chunks = 2 * CHUNKS

    def panel_step(j):
        up = j - AHEAD * c

        @pl.when((up >= 0) & (up < total_chunks))
        def _():
            s, k = lax.div(up, CHUNKS), lax.rem(up, CHUNKS)

            @pl.when(c > 0)
            def _():
                plus_copy(s, k).wait_recv()
                plus[s, chunk(k), :] = plus[s, chunk(k), :] + own(s, k)

            @pl.when(c == 0)
            def _():
                plus[s, chunk(k), :] = own(s, k)

            @pl.when(c < end)
            def _():
                plus_copy(s, k).start()

        down = j - AHEAD * (end - c)

        @pl.when((down >= 0) & (down < total_chunks))
        def _():
            s, k = lax.div(down, CHUNKS), lax.rem(down, CHUNKS)

            @pl.when(c < end)
            def _():
                minus_copy(s, k).wait_recv()
                minus[s, chunk(k), :] = minus[s, chunk(k), :] + own(s, k)

            @pl.when(c == end)
            def _():
                minus[s, chunk(k), :] = own(s, k)

            @pl.when(c > 0)
            def _():
                minus_copy(s, k).start()

        at = j - AHEAD * end

        @pl.when(at >= 0)
        def _():
            s, k = lax.div(at, CHUNKS), lax.rem(at, CHUNKS)
            x = (plus[s, chunk(k), :] + minus[s, chunk(k), :]) - own(s, k)
            bf[s, chunk(k), :] = x
            high, rest_ = halves(x)
            bh[s, chunk(k), :] = high
            bl[s, chunk(k), :] = rest_

    def reduce_events(g, src, bufs, dst, apart, offset, first_size, finish):
        size = [None] + [first_size >> j for j in range(bits)]
        start = [None, value[0] * apart + offset]
        for j in range(1, bits):
            start.append(start[-1] + value[j] * size[j + 1])

        def away(j):
            if j == 0:
                return (1 - value[0]) * apart + offset
            return start[j] + (1 - value[j]) * size[j + 1]

        def rs(j):
            return remote(src.at[span(away(j), size[j + 1]), :], bufs[j],
                          rs_s.at[g, j], rs_r.at[g, j], {"row": partner[j]})

        def ag(j):
            if j == 0:
                mine = span(start[1], size[1])
            else:
                mine = span(start[j + 1], size[j + 1])
            return remote(dst.at[mine, :], dst.at[mine, :],
                          ag_s.at[g, j], ag_r.at[g, j], {"row": partner[j]})

        def add(j):
            rs(j).wait()
            mine = size[j + 1]
            piece = min(mine, 128)

            def body(i):
                here = span(start[j + 1] + i * piece, piece)
                src[here, :] = src[here, :] + bufs[j][span(i * piece, piece), :]
            loop(0, mine // piece, body)

        def event(i):
            if i == 0:
                rs(0).start()
            elif i < bits:
                add(i - 1)
                rs(i).start()
            elif i == bits:
                add(bits - 1)
                finish(start[bits], size[bits])
                ag(bits - 1).start()
            else:
                j = 2 * bits - i
                ag(j).wait()
                if j > 0:
                    ag(j - 1).start()
        return [functools.partial(event, i) for i in range(2 * bits + 1)]

    def finish_column(s, start, size):
        piece = min(size, width, 128)

        def body(i):
            at = start + i * piece
            block = lax.div(c * rows + at, width)
            here = span(at, piece)
            y[s, here, :] = sign_ref[s, block] * part[s, here, :]
        loop(0, size // piece, body)

    source = lax.div(r * n_cols, n_rows)
    own_start = r * depth - source * rows
    parts = [[k for k in range(CHUNKS) if (k * ch // strip) % 2 == h] for h in range(2)]

    def z_copy(s, k, src, way):
        sem = zl_s if way < 0 else zr_s
        return remote(src, low.at[s, chunk(k), :], sem.at[s, k], z_r.at[s, k],
                      left if way < 0 else right)

    def z_send(s, k, src):
        @pl.when((c <= source) & (c > 0))
        def _():
            z_copy(s, k, src, -1).start()

        @pl.when((c >= source) & (c < end))
        def _():
            z_copy(s, k, src, 1).start()

    def z_root(s, h):
        @pl.when(c == source)
        def _():
            for k in parts[h]:
                z_send(s, k, y.at[s, span(own_start + k * ch, ch), :])
            for k in parts[h]:
                low[s, chunk(k), :] = y[s, span(own_start + k * ch, ch), :]

    def z_relay(s, k):
        @pl.when(c != source)
        def _():
            z_copy(s, k, low.at[s, chunk(k), :], 1).wait_recv()
            z_send(s, k, low.at[s, chunk(k), :])

    def low_copy(s):
        return pltpu.make_async_copy(low.at[s], low_out.at[s], o_sem.at[s])

    tb = rows // 8

    def turn_copy(i):
        s, b = i // 8, i % 8
        return pltpu.make_async_copy(
            turned.at[i % 2], y_out.at[s, :, pl.ds(b * tb, tb)], t_sem.at[i % 2]
        )

    def turn(i):
        s, b = i // 8, i % 8
        if i >= 2:
            turn_copy(i - 2).wait()
        turned[i % 2] = y[s, pl.ds(b * tb, tb), :].T
        turn_copy(i).start()

    def inner(s, k):
        b = halves(bf[s, chunk(k), :].T)
        dpart[s] += dot3(b, halves(low[s, chunk(k), :]))

    barrier = pltpu.get_barrier_semaphore()
    for j in range(bits):
        pl.semaphore_signal(barrier, inc=1, device_id={"row": partner[j]}, device_id_type=MESH)

    @pl.when(c > 0)
    def _():
        pl.semaphore_signal(barrier, inc=1, device_id=left, device_id_type=MESH)

    @pl.when(c < end)
    def _():
        pl.semaphore_signal(barrier, inc=1, device_id=right, device_id_type=MESH)

    beside = lax.div(c + end - 1, end) + lax.div(2 * end - 1 - c, end)
    pl.semaphore_wait(barrier, bits + beside)

    a_copy(0)[2].start()
    dpart[...] = jnp.zeros_like(dpart)

    def column_events(s, h):
        g = 2 * s + h
        return reduce_events(g, part.at[s], [b.at[g] for b in rs_buf], y.at[s],
                             rows // 2, h * strip, strip, functools.partial(finish_column, s))

    def diag_events(s):
        def finish(start, size):
            here = span(start, size)
            dsum[s, here, :] = dpart[s, here, :]
        return reduce_events(4 + s, dpart.at[s], [b.at[s] for b in d_buf], dsum.at[s],
                             width // 2, 0, width // 2, finish)

    events = {(s, h): column_events(s, h) for s in range(2) for h in range(2)}
    root = {key: functools.partial(z_root, *key) for key in events}
    ready = CHUNKS + AHEAD * end
    quarter = TILES // 4

    loop(0, ready, panel_step)
    per = CHUNKS // 2 // 4
    for q in range(4):
        def both(i, q=q):
            panel_step(ready + q * per + i)
            each = quarter // per
            loop(0, each, lambda m: multiply(0, q * quarter + i * each + m))
        loop(0, per, both)
        e, f = events[0, 0], events[0, 1]
        for event in ([e[0]], [e[1]], [f[0]], [e[2], f[1]])[q]:
            event()
    steps = [functools.partial(panel_step, ready + 4 * per + i) for i in range(CHUNKS - 4 * per)]
    e, f = events[0, 0][3:] + [root[0, 0]], events[0, 1][2:] + [root[0, 1]]
    late = 2
    for step in weave(steps, weave(e, f[:-late])):
        step()
    order = parts[0] + parts[1]
    relays = [functools.partial(z_relay, 0, k) for k in order]
    for q in range(4):
        loop(0, quarter, lambda m: multiply(1, q * quarter + m))
        e, g = events[1, 0], events[1, 1]
        if q == 0:
            todo = f[-late:] + [e[0]]
        else:
            todo = relays[:2] + [[], [e[1]], [g[0]], [e[2], g[1]]][q]
            relays = relays[2:]
        for event in todo:
            event()
    e, g = events[1, 0][3:] + [root[1, 0]], events[1, 1][2:] + [root[1, 1]]
    for step in weave(weave(e, g), relays):
        step()
    low_copy(0).start()
    inners = [functools.partial(loop, i * CHUNKS // 4, (i + 1) * CHUNKS // 4,
                                lambda k: inner(0, k)) for i in range(4)]
    side = weave(inners + diag_events(0), [functools.partial(turn, i) for i in range(16)])

    def last(k):
        z_relay(1, k)
        inner(1, k)
    for step in weave([functools.partial(last, k) for k in order], side):
        step()
    low_copy(1).start()
    for event in diag_events(1):
        event()
    diag_out[...] = dinv_ref[...] - dsum[...]

    for s in range(2):
        def drain(k, s=s):
            @pl.when(c < end)
            def _():
                plus_copy(s, k).wait_send()

            @pl.when(c > 0)
            def _():
                minus_copy(s, k).wait_send()

            src = low.at[s, chunk(k), :]

            @pl.when((c <= source) & (c > 0))
            def _():
                z_copy(s, k, src, -1).wait_send()

            @pl.when((c >= source) & (c < end))
            def _():
                z_copy(s, k, src, 1).wait_send()
        loop(0, CHUNKS, drain)
    turn_copy(14).wait()
    turn_copy(15).wait()
    for s in range(2):
        low_copy(s).wait()


def exchange(n_rows, n_cols, a, panel, scale, sign, dinv):
    rows, depth = a.shape
    width = panel.shape[1]
    bits = n_rows.bit_length() - 1
    vmem = pl.BlockSpec(memory_space=pltpu.VMEM)
    smem = pl.BlockSpec(memory_space=pltpu.SMEM)
    anywhere = pl.BlockSpec(memory_space=pl.ANY)
    dma = pltpu.SemaphoreType.DMA
    n = CHUNKS
    return pl.pallas_call(
        functools.partial(kernel, n_rows, n_cols),
        out_shape=(
            jax.ShapeDtypeStruct((2, width, rows), F32),
            jax.ShapeDtypeStruct((2, depth, width), F32),
            jax.ShapeDtypeStruct((2, width, width), F32),
        ),
        in_specs=[anywhere, vmem, smem, smem, vmem],
        out_specs=(anywhere, anywhere, vmem),
        scratch_shapes=[
            pltpu.VMEM((2, depth, width), F32),
            pltpu.VMEM((2, depth, width), BF16),
            pltpu.VMEM((2, depth, width), BF16),
            pltpu.VMEM((2, depth, width), F32),
            pltpu.VMEM((2, depth, width), F32),
            pltpu.VMEM((2, rows, width), F32),
            pltpu.VMEM((2, rows, width), F32),
            pltpu.VMEM((2, depth, width), F32),
            pltpu.VMEM((2, rows // TILES, depth), F32),
            pltpu.VMEM((2, width, rows // 8), F32),
            pltpu.VMEM((2, width, width), F32),
            pltpu.VMEM((2, width, width), F32),
            *[pltpu.VMEM((4, rows // 4 >> j, width), F32) for j in range(bits)],
            *[pltpu.VMEM((2, width // 2 >> j, width), F32) for j in range(bits)],
            dma((2, n)), dma((2, n)), dma((2, n)), dma((2, n)),
            dma((6, bits)), dma((6, bits)), dma((6, bits)), dma((6, bits)),
            dma((2, n)), dma((2, n)), dma((2, n)),
            dma((2,)), dma((2,)), dma((2,)),
        ],
        compiler_params=pltpu.CompilerParams(
            collective_id=0, has_side_effects=True, vmem_limit_bytes=66_000_000
        ),
    )(a, panel, scale, sign, dinv)


def shards(inverse_rows, panels, diag_inverse, pattern, owner_slot):
    live = pattern.astype(F32)
    mine = (owner_slot == lax.axis_index("col")).astype(F32)
    y, low, diag = exchange(
        lax.axis_size("row"), lax.axis_size("col"), inverse_rows, panels[0],
        live * mine[:, None], -live, diag_inverse,
    )
    return low, y, diag


def solution(mesh):
    in_specs = (P("col", "row"), P("col", "row", None), P(), P(), P())
    out_specs = (P(None, "row", None), P(None, None, "col"), P())
    return jax.shard_map(shards, mesh=mesh, in_specs=in_specs, out_specs=out_specs, check_vma=False)
```
